256 devices in a mesh: seq: 64 (over x, z, core), ctx: 4 (over y).
Axes of the slice: x: 4, y: 4, z: 8, core: 2. Of those that a mesh axis runs over, the one named last changes fastest.
Arguments:
- queries: bfloat16 [4096, 8192], P(('seq', 'ctx'))
- new_token_keys: bfloat16 [4096, 1024], P(('seq', 'ctx'))
- new_token_values: bfloat16 [4096, 1024], P(('seq', 'ctx')), may hold values from -0.796875 to 0.796875
- cache_keys: bfloat16 [64, 32768, 128], P('seq', 'ctx'), as said below
- cache_values: bfloat16 [64, 32768, 128], P('seq', 'ctx'), as said below
- block_ids: int32 [64, 64, 4, 12], P('seq', None, 'ctx'), may hold values from 0 to 63, as said below
- block_counts: int32 [64, 64, 4], P('seq', None, 'ctx'), may hold values from 1 to 12, as said below
Outputs:
- attended: bfloat16 [4096, 8192], P(('seq', 'ctx'))
The draws below stay inside these ranges and needn't reach their ends.
Inputs may be any that keep to these rules, and one draw needn't show every extreme that they name: `block_ids`: within one list of 12 entries the key blocks are distinct; only the first block_counts of them are used. `block_counts`: the most, 12, is reached in every draw. cache_keys[h] equals cache_keys[h2] where floor(h / 8) = floor(h2 / 8). cache_values[h] equals cache_values[h2] where floor(h / 8) = floor(h2 / 8).
All inputs are finite; a program needn't handle non-finite values.
Results may differ from the reference program's by a relative error of at most 0.0075.
Values may be sent and summed in bfloat16 or wider, within the bound.
A program may use at most 64 MiB of HBM per device.

```python
import math
import jax
import jax.numpy as jnp
from jax import lax

HEAD_WIDTH = 128
HEADS_PER_GROUP = 8
TILE_QUERY_ROWS = 64
KROWS = 128
KQ = 12
CTX_DEV = 8192
QUERY_HEAD_COUNT = 64
KEY_VALUE_HEADS = 8
NEW_TOKENS = 4096
CACHED_TOKENS = 32768
QB = 64
KBQ = 64
N_CTX = 4


def listed_blocks(key):
    cache_quarters = CACHED_TOKENS // CTX_DEV
    ranking = jax.random.randint(key, (QUERY_HEAD_COUNT, QB, cache_quarters, KBQ), 0, 2 ** 20) * KBQ + jnp.arange(KBQ, dtype=jnp.int32)
    order = jnp.argsort(ranking, axis=-1, stable=True)
    return order[..., :KQ].astype(jnp.int32)


def cache_common(key, salt, dispersed):
    provider = jax.random.fold_in(key, salt)
    unscaled = dispersed * jax.random.normal(provider, (KEY_VALUE_HEADS, CACHED_TOKENS, HEAD_WIDTH), jnp.float32)
    return jnp.repeat(unscaled.astype(jnp.bfloat16), HEADS_PER_GROUP, axis=0)


def draw_cache_keys(key, part):
    return cache_common(key, 301, 1.5)


def draw_cache_values(key, part):
    return cache_common(key, 302, 0.45)


def simple_rows(provider, columns):
    return 1.5 * jax.random.normal(provider, (NEW_TOKENS, columns), jnp.float32)


def draw_queries(key, part):
    final_output = simple_rows(jax.random.fold_in(key, 401), QUERY_HEAD_COUNT * HEAD_WIDTH)
    return final_output.astype(jnp.bfloat16)


def draw_new_token_keys(key, part):
    final_output = simple_rows(jax.random.fold_in(key, 402), KEY_VALUE_HEADS * HEAD_WIDTH)
    return final_output.astype(jnp.bfloat16)


def draw_block_ids(key, part):
    return listed_blocks(key)


def draw_block_counts(key, part):
    cache_quarters = CACHED_TOKENS // CTX_DEV
    upper = jax.random.randint(jax.random.fold_in(key, 601), (QUERY_HEAD_COUNT, 1, cache_quarters), max(1, KQ // 2), KQ + 1)
    lower = jnp.maximum(1, upper // 2)
    counts = jax.random.randint(jax.random.fold_in(key, 602), (QUERY_HEAD_COUNT, QB, cache_quarters), lower, upper + 1)
    where_full = jax.random.randint(jax.random.fold_in(key, 603), (), 0, QUERY_HEAD_COUNT * QB * cache_quarters)
    counts = counts.reshape(-1).at[where_full].set(KQ).reshape(QUERY_HEAD_COUNT, QB, cache_quarters)
    return counts.astype(jnp.int32)


def block_levels(stream_key, extent, cuts, low, largest):
    def one(dim, blocks):
        draws = jax.random.uniform(jax.random.fold_in(jax.random.fold_in(stream_key, 6), dim), (blocks,), jnp.float32, low / len(cuts), largest / len(cuts))
        return jnp.repeat(jnp.exp(draws), extent[dim] // blocks).reshape((-1,) + (1,) * (len(extent) - dim - 1))

    loudness = one(*cuts[0])
    for cut in cuts[1:]:
        loudness = loudness * one(*cut)
    return loudness


def setup_inputs(seed: int = 0) -> dict:
    streams_of = jax.random.split(jax.random.key(seed), 8)
    queries = draw_queries(jax.random.fold_in(streams_of[7], 71), 0)
    new_token_keys = draw_new_token_keys(jax.random.fold_in(streams_of[7], 71), 0)
    new_token_values = jnp.clip(jax.random.uniform(streams_of[2], (NEW_TOKENS, KEY_VALUE_HEADS * HEAD_WIDTH), jnp.float32, -0.796875, 0.796875) * block_levels(streams_of[2], (NEW_TOKENS, KEY_VALUE_HEADS * HEAD_WIDTH), ((0, 256),), -0.4, 0.0), -0.796875, 0.796875).astype(jnp.bfloat16)
    cache_keys = draw_cache_keys(jax.random.fold_in(streams_of[7], 71), 0)
    cache_values = draw_cache_values(jax.random.fold_in(streams_of[7], 71), 0)
    block_ids = draw_block_ids(jax.random.fold_in(streams_of[7], 71), 0)
    block_counts = draw_block_counts(jax.random.fold_in(streams_of[7], 71), 0)
    return dict(queries=queries, new_token_keys=new_token_keys, new_token_values=new_token_values, cache_keys=cache_keys, cache_values=cache_values, block_ids=block_ids, block_counts=block_counts)


def head_attend(query_head, key_head, value_head, cached_keys, cached_values, listed, used):
    tile_keys = cached_keys.reshape(N_CTX * KBQ, KROWS, HEAD_WIDTH)
    tile_values = cached_values.reshape(N_CTX * KBQ, KROWS, HEAD_WIDTH)
    offsets = jnp.arange(N_CTX, dtype=jnp.int32)[None, :, None] * KBQ
    global_ids = (offsets + listed).reshape(QB, N_CTX * KQ)
    selected_keys = tile_keys[global_ids].reshape(QB, N_CTX * KQ * KROWS, HEAD_WIDTH)
    picked_values = tile_values[global_ids].reshape(QB, N_CTX * KQ * KROWS, HEAD_WIDTH)
    slot_ok = (jnp.arange(KQ, dtype=jnp.int32)[None, None, :] < used[:, :, None]).reshape(QB, N_CTX * KQ)
    slot_ok = jnp.repeat(slot_ok, KROWS, axis=1)
    padded_keys = jnp.concatenate([jnp.zeros((KROWS, HEAD_WIDTH), jnp.bfloat16), key_head]).reshape(NEW_TOKENS // KROWS + 1, KROWS, HEAD_WIDTH)
    padded_values = jnp.concatenate([jnp.zeros((KROWS, HEAD_WIDTH), jnp.bfloat16), value_head]).reshape(NEW_TOKENS // KROWS + 1, KROWS, HEAD_WIDTH)
    block_index = jnp.arange(QB, dtype=jnp.int32)
    key_block = block_index * TILE_QUERY_ROWS // KROWS
    nearby_keys = jnp.concatenate([padded_keys[key_block], padded_keys[key_block + 1]], axis=1)
    near_values = jnp.concatenate([padded_values[key_block], padded_values[key_block + 1]], axis=1)
    positions = (key_block[:, None] - 1) * KROWS + jnp.arange(2 * KROWS, dtype=jnp.int32)[None, :]
    query_pos = block_index[:, None] * TILE_QUERY_ROWS + jnp.arange(TILE_QUERY_ROWS, dtype=jnp.int32)[None, :]
    near_ok = (positions[:, None, :] >= 0) & (positions[:, None, :] <= query_pos[:, :, None])
    every_key = jnp.concatenate([selected_keys, nearby_keys], axis=1)
    every_value = jnp.concatenate([picked_values, near_values], axis=1)
    visible = jnp.concatenate([jnp.broadcast_to(slot_ok[:, None, :], (QB, TILE_QUERY_ROWS, N_CTX * KQ * KROWS)), near_ok], axis=2)
    tiled_queries = query_head.reshape(QB, TILE_QUERY_ROWS, HEAD_WIDTH)
    logit_scores = jnp.einsum('pmt,pyt->pmy', tiled_queries.astype(jnp.float32), every_key.astype(jnp.float32)) * (1.0 / math.sqrt(HEAD_WIDTH))
    top = lax.optimization_barrier(jnp.max(jnp.where(visible, logit_scores, -jnp.inf), axis=-1, keepdims=True))
    exponent_terms = jnp.where(visible, jnp.exp(logit_scores - top), jnp.float32(0.0))
    totals = lax.optimization_barrier(jnp.sum(exponent_terms, axis=-1, keepdims=True))
    attention_weights = exponent_terms.astype(jnp.bfloat16)
    blended = jnp.einsum('nst,ntw->nsw', attention_weights.astype(jnp.float32), every_value.astype(jnp.float32))
    return (blended / totals).astype(jnp.bfloat16).reshape(NEW_TOKENS, HEAD_WIDTH)

def reference(queries, new_token_keys, new_token_values, cache_keys, cache_values, block_ids, block_counts):
    query_stack = queries.reshape(NEW_TOKENS, QUERY_HEAD_COUNT, HEAD_WIDTH).transpose(1, 0, 2)
    stacked_keys = new_token_keys.reshape(NEW_TOKENS, KEY_VALUE_HEADS, HEAD_WIDTH).transpose(1, 0, 2)
    stacked_values = new_token_values.reshape(NEW_TOKENS, KEY_VALUE_HEADS, HEAD_WIDTH).transpose(1, 0, 2)
    head_index = jnp.arange(QUERY_HEAD_COUNT, dtype=jnp.int32)

    def one_head(operands):
        query_head, cached_keys, cached_values, listed, used, index = operands
        kv_index = index // HEADS_PER_GROUP
        key_head = lax.dynamic_index_in_dim(stacked_keys, kv_index, 0, keepdims=False)
        value_head = lax.dynamic_index_in_dim(stacked_values, kv_index, 0, keepdims=False)
        return head_attend(query_head, key_head, value_head, cached_keys, cached_values, listed, used)
    outputs = lax.map(one_head, (query_stack, cache_keys, cache_values, block_ids, block_counts, head_index))
    return outputs.transpose(1, 0, 2).reshape(NEW_TOKENS, QUERY_HEAD_COUNT * HEAD_WIDTH)
```

```python
import math

import jax
import jax.numpy as jnp
from jax import lax
from jax.experimental import pallas as pl
from jax.experimental.pallas import tpu as pltpu
from jax.sharding import PartitionSpec as P

HEADS = 8
ROWS = 64
KROWS = 128
KQ = 12
D = 128
NB = 8
CTX = 4
ZS = 8
PIECE = ROWS // CTX
WIDE = HEADS * D
MSG = WIDE + D
LAG = 2
C = math.log2(math.e) / math.sqrt(D)
NT = (((1,), (1,)), ((), ()))
MESH = pl.DeviceIdType.MESH
F32, BF16 = jnp.float32, jnp.bfloat16


def member(z, group):
    near_z = jnp.minimum(z, ZS - 1 - z)
    return 2 * jnp.where(group % 2 == 0, near_z, 3 - near_z) + jnp.where(z >= 4, 1, 0)


def z_of(e, group):
    near_z = jnp.where(group % 2 == 0, e // 2, 3 - e // 2)
    return jnp.where(e % 2 == 0, near_z, ZS - 1 - near_z)


def kernel(
    q_hbm, nk_hbm, nv_hbm, k_hbm, v_hbm, tbl_hbm, out_hbm,
    q_buf, k_buf, v_buf, nks, nvs, kvs, kvn, tbl_buf, tbl, s_buf, acc, lse, nacc, nlse, msg, rcv, fin,
    load_sem, q_send, q_recv, y_send, y_recv, kv_send, kv_recv, t_send, t_recv, m_send, m_recv, f_send, f_recv, smem_sem,
):
    s, c = lax.axis_index("seq"), lax.axis_index("ctx")
    x, z, core = s // 16, (s // 2) % ZS, s % 2
    group, e = s // HEADS, s % HEADS
    zt = z_of(e, group)
    mine = x * 2 + core

    loads = [
        pltpu.make_async_copy(nk_hbm, nks, load_sem.at[0]),
        pltpu.make_async_copy(nv_hbm, nvs, load_sem.at[1]),
        pltpu.make_async_copy(k_hbm, k_buf, load_sem.at[2]),
        pltpu.make_async_copy(v_hbm, v_buf, load_sem.at[3]),
    ]
    for load in loads:
        load.start()

    def signal(seq, ctx):
        pl.semaphore_signal(barrier, inc=1, device_id=(seq, ctx), device_id_type=MESH)

    barrier = pltpu.get_barrier_semaphore()
    expected = jnp.int32(7 + 3)
    for j in range(1, CTX):
        signal(s, (c + j) % CTX)
    for j in range(1, HEADS):
        signal(group * HEADS + (e + j) % HEADS, c)
    for n in range(NB):
        seq = ((n // 2) * ZS + zt) * 2 + n % 2
        pl.when(seq != s)(lambda seq=seq: signal(seq, c))
    near_b = c * ZS + zt
    for role in range(2):
        for i in range(8):
            seq, ctx = (near_b - role) * 2 + i % 2, i // 2
            ok = (near_b - role >= 0) & ((seq != s) | (ctx != c))
            pl.when(ok)(lambda seq=seq, ctx=ctx: signal(seq, ctx))

    def q_dest(g):
        return g * HEADS + member(z, g)

    def kv_dest(role, g):
        b = x * ZS + z + role
        return g * HEADS + member(b % ZS, g), b // ZS

    for g in range(8):
        expected += jnp.where(q_dest(g) != s, 1, 0)
        for role in range(2):
            seq, ctx = kv_dest(role, g)
            expected += jnp.where((ctx < CTX) & ((seq != s) | (ctx != c)), 1, 0)

    loads[0].wait()
    loads[1].wait()
    for g in range(8):
        kvs[g, :, :D] = nks[:, g * D:(g + 1) * D]
        kvs[g, :, D:] = nvs[:, g * D:(g + 1) * D]

    @pl.when(near_b == 0)
    def _():
        kvn[:KROWS] = jnp.zeros((KROWS, 2 * D), BF16)

    pl.semaphore_wait(barrier, expected)

    def remote(src, dst, send, recv, seq, ctx):
        return pltpu.make_async_remote_copy(
            src_ref=src, dst_ref=dst, send_sem=send, recv_sem=recv, device_id=(seq, ctx), device_id_type=MESH
        )

    def t_copy(j):
        to = (e + j) % HEADS
        return remote(
            tbl_hbm.at[z_of(to, group)], tbl_buf.at[e], t_send.at[j], t_recv, group * HEADS + to, c
        )

    t_own = pltpu.make_async_copy(tbl_hbm.at[zt], tbl_buf.at[e], t_recv)
    t_own.start()
    for j in range(1, HEADS):
        t_copy(j).start()

    rows_c = pl.ds(pl.multiple_of(c * PIECE, PIECE), PIECE)

    def q_copy(g):
        src, dst = q_hbm.at[:, pl.ds(g * WIDE, WIDE)], q_buf.at[mine, rows_c]
        return (
            remote(src, dst, q_send.at[g], q_recv.at[mine], q_dest(g), c),
            pltpu.make_async_copy(src, dst, q_recv.at[mine]),
        )

    def start_either(copies, own):
        pl.when(own)(copies[1].start)
        pl.when(jnp.logical_not(own))(copies[0].start)

    for g in range(8):
        start_either(q_copy(g), q_dest(g) == s)

    def kv_copy(role, g):
        seq, ctx = kv_dest(role, g)
        row = (1 - role) * KROWS + core * ROWS + c * PIECE
        dst = kvn.at[pl.ds(pl.multiple_of(row, PIECE), PIECE)]
        own = (seq == s) & (ctx == c)
        return (
            remote(kvs.at[g], dst, kv_send.at[role * 8 + g], kv_recv, seq, ctx),
            pltpu.make_async_copy(kvs.at[g], dst, kv_recv),
            own,
            (ctx < CTX) & jnp.logical_not(own),
        )

    for role in range(2):
        for g in range(8):
            there, here, own, other = kv_copy(role, g)
            pl.when(own)(here.start)
            pl.when(other)(there.start)

    def landed(ref, sem):
        pltpu.make_async_copy(ref, ref, sem).wait()

    def y_copy(n, j):
        piece = q_buf.at[n, rows_c]
        return remote(piece, piece, y_send.at[j - 1, n], y_recv.at[j - 1, n], s, (c + j) % CTX)

    def forward(n, _):
        landed(q_buf.at[n, rows_c], q_recv.at[n])
        for j in range(1, CTX):
            y_copy(n, j).start()
        return 0

    lax.fori_loop(0, NB, forward, 0)

    landed(tbl_buf, t_recv)
    to_smem = pltpu.make_async_copy(tbl_buf, tbl, smem_sem)
    to_smem.start()
    loads[2].wait()
    loads[3].wait()
    to_smem.wait()

    lane = lax.broadcasted_iota(jnp.int32, (1, D), 1)

    def finish(o, l, m, h, o_ref, total):
        o_ref[:, h * D:(h + 1) * D] = o * (1.0 / l)
        return jnp.where(lane % HEADS == h, m + jnp.log2(l), total)

    def near(n):
        @pl.when(n % 2 == 0)
        def _():
            pl.when(near_b > 0)(lambda: landed(kvn, kv_recv))
            pl.when(near_b == 0)(lambda: landed(kvn.at[pl.ds(KROWS, KROWS)], kv_recv))

        key = lax.broadcasted_iota(jnp.int32, (ROWS, 2 * KROWS), 1)
        row = lax.broadcasted_iota(jnp.int32, (ROWS, 2 * KROWS), 0)
        first = jnp.where(near_b > 0, 0, KROWS)
        visible = (key >= first) & (key <= row + (KROWS + (n % 2) * ROWS))
        total = jnp.zeros((ROWS, D), F32)
        for h in range(HEADS):
            sc = lax.dot_general(q_buf[n, :, h * D:(h + 1) * D], kvn[:, :D], NT, preferred_element_type=F32)
            sc = jnp.where(visible, sc * C, -jnp.inf)
            m = jnp.max(sc, axis=1, keepdims=True)
            p = jnp.exp2(sc - m)
            l = jnp.sum(p, axis=1, keepdims=True)
            o = jnp.dot(p.astype(BF16), kvn[:, D:], preferred_element_type=F32)
            total = finish(o, l, m, h, nacc, total)
        nlse[...] = total

    def attend(n):
        tops = []
        for h in range(HEADS):
            qq = q_buf[n, :, h * D:(h + 1) * D]
            m = jnp.full((ROWS, KROWS), -jnp.inf, F32)
            for t in range(0, KQ, 2):
                kk = jnp.concatenate([k_buf[tbl[h, n, t + i]] for i in range(2)], 0)
                sc = lax.dot_general(qq, kk, NT, preferred_element_type=F32)
                s_buf[h, :, t * KROWS:(t + 2) * KROWS] = sc
                m = jnp.maximum(m, jnp.maximum(sc[:, :KROWS], sc[:, KROWS:]))
            tops.append(jnp.max(m, axis=1, keepdims=True) * C)
        total = jnp.zeros((ROWS, D), F32)
        for h in range(HEADS):
            used, m = tbl[h, n, KQ], tops[h]
            o = jnp.zeros((ROWS, D), F32)
            l = jnp.zeros((ROWS, KROWS), F32)
            for t in range(0, KQ, 2):
                parts = []
                for i in range(2):
                    shift = m + jnp.where(t + i < used, 0.0, jnp.inf)
                    p = jnp.exp2(s_buf[h, :, (t + i) * KROWS:(t + i + 1) * KROWS] * C - shift)
                    l = l + p
                    parts.append(p.astype(BF16))
                vv = jnp.concatenate([v_buf[tbl[h, n, t + i]] for i in range(2)], 0)
                o = o + jnp.dot(jnp.concatenate(parts, 1), vv, preferred_element_type=F32)
            total = finish(o, jnp.sum(l, axis=1, keepdims=True), m, h, acc, total)
        lse[...] = total

    def merge_near():
        top = jnp.maximum(lse[...], nlse[...])
        w0, w1 = jnp.exp2(lse[...] - top), jnp.exp2(nlse[...] - top)
        both = w0 + w1
        w0, w1 = w0 / both, w1 / both
        for h in range(HEADS):
            cols = slice(h * D, (h + 1) * D)
            acc[:, cols] = acc[:, cols] * w0[:, h:h + 1] + nacc[:, cols] * w1[:, h:h + 1]
        lse[...] = top + jnp.log2(both)

    def pack(n):
        for h in range(HEADS):
            msg[n, :, h * D:(h + 1) * D] = acc[:, h * D:(h + 1) * D].astype(BF16)
        full = lse[...]
        one = full.astype(BF16)
        rest = full - one.astype(F32)
        two = rest.astype(BF16)
        three = (rest - two.astype(F32)).astype(BF16)
        terms = jnp.where(lane < HEADS, one.astype(F32), jnp.where(lane < 2 * HEADS, two.astype(F32), three.astype(F32)))
        msg[n, :, WIDE:] = terms.astype(BF16)

    def m_copy(n, j):
        to = (c + j) % CTX
        src = msg.at[n, pl.ds(pl.multiple_of(to * PIECE, PIECE), PIECE)]
        return remote(src, rcv.at[j - 1, n], m_send.at[j - 1, n], m_recv.at[j - 1, n], s, to)

    def f_seq(n):
        return ((n // 2) * ZS + zt) * 2 + n % 2

    def f_copy(n):
        dst = out_hbm.at[:, pl.ds(pl.multiple_of(group * WIDE, WIDE), WIDE)]
        return (
            remote(fin.at[n], dst, f_send.at[n], f_recv, f_seq(n), c),
            pltpu.make_async_copy(fin.at[n], dst, f_recv),
        )

    def join(n):
        for j in range(1, CTX):
            landed(rcv.at[j - 1, n], m_recv.at[j - 1, n])
        parts = [msg.at[n, rows_c]] + [rcv.at[j, n] for j in range(CTX - 1)]
        logs = []
        for part in parts:
            terms = part[:, WIDE:].astype(F32)
            logs.append(terms + pltpu.roll(terms, D - HEADS, 1) + pltpu.roll(terms, D - 2 * HEADS, 1))
        top = jnp.maximum(jnp.maximum(logs[0], logs[1]), jnp.maximum(logs[2], logs[3]))
        weights = [jnp.exp2(log - top) for log in logs]
        inverse = 1.0 / (weights[0] + weights[1] + weights[2] + weights[3])
        weights = [w * inverse for w in weights]
        for h in range(HEADS):
            cols = slice(h * D, (h + 1) * D)
            o = sum(part[:, cols].astype(F32) * w[:, h:h + 1] for part, w in zip(parts, weights))
            fin[n, :, cols] = o.astype(BF16)
        start_either(f_copy(n), f_seq(n) == s)

    def step(n, _):
        @pl.when(n < NB)
        def _():
            for j in range(1, CTX):
                rows = pl.ds(pl.multiple_of(((c + CTX - j) % CTX) * PIECE, PIECE), PIECE)
                landed(q_buf.at[n, rows], y_recv.at[j - 1, n])
            is_near = n // 2 == c
            pl.when(is_near)(lambda: near(n))
            attend(n)
            pl.when(is_near)(merge_near)
            pack(n)
            for j in range(1, CTX):
                m_copy(n, j).start()

        pl.when(n >= LAG)(lambda: join(n - LAG))
        return 0

    lax.fori_loop(0, NB + LAG, step, 0)

    for j in range(1, HEADS):
        t_copy(j).wait_send()
    for g in range(8):
        pl.when(q_dest(g) != s)(q_copy(g)[0].wait_send)
        for role in range(2):
            there, _, _, other = kv_copy(role, g)
            pl.when(other)(there.wait_send)

    def drain(n, _):
        for j in range(1, CTX):
            y_copy(n, j).wait_send()
            m_copy(n, j).wait_send()
        pl.when(f_seq(n) != s)(f_copy(n)[0].wait_send)
        return 0

    lax.fori_loop(0, NB, drain, 0)
    landed(out_hbm, f_recv)


def body(queries, new_token_keys, new_token_values, cache_keys, cache_values, block_ids, block_counts):
    used = block_counts[0, :, :]
    slot = jnp.arange(KQ, dtype=jnp.int32)[None, :]
    ids = block_ids[0, :, 0, :]
    ids = jnp.where(slot < used, ids, ids[:, :1])
    table = jnp.concatenate([ids, used, jnp.zeros((ids.shape[0], D - KQ - 1), jnp.int32)], axis=1)
    table = table.reshape(CTX, ZS, 2, D).transpose(1, 0, 2, 3).reshape(ZS, NB, D)
    blocks = cache_keys.shape[1] // KROWS
    hbm = pl.BlockSpec(memory_space=pl.ANY)
    dma = pltpu.SemaphoreType.DMA
    return pl.pallas_call(
        kernel,
        out_shape=jax.ShapeDtypeStruct(queries.shape, BF16),
        in_specs=[hbm] * 6,
        out_specs=hbm,
        scratch_shapes=[
            pltpu.VMEM((NB, ROWS, WIDE), BF16),
            pltpu.VMEM((blocks, KROWS, D), BF16),
            pltpu.VMEM((blocks, KROWS, D), BF16),
            pltpu.VMEM((PIECE, WIDE), BF16),
            pltpu.VMEM((PIECE, WIDE), BF16),
            pltpu.VMEM((8, PIECE, 2 * D), BF16),
            pltpu.VMEM((2 * KROWS, 2 * D), BF16),
            pltpu.VMEM((HEADS, NB, D), jnp.int32),
            pltpu.SMEM((HEADS, NB, D), jnp.int32),
            pltpu.VMEM((HEADS, ROWS, KQ * KROWS), F32),
            pltpu.VMEM((ROWS, WIDE), F32),
            pltpu.VMEM((ROWS, D), F32),
            pltpu.VMEM((ROWS, WIDE), F32),
            pltpu.VMEM((ROWS, D), F32),
            pltpu.VMEM((NB, ROWS, MSG), BF16),
            pltpu.VMEM((CTX - 1, NB, PIECE, MSG), BF16),
            pltpu.VMEM((NB, PIECE, WIDE), BF16),
            dma((4,)), dma((8,)), dma((NB,)), dma((CTX - 1, NB)), dma((CTX - 1, NB)), dma((16,)), dma, dma((HEADS,)), dma,
            dma((CTX - 1, NB)), dma((CTX - 1, NB)), dma((NB,)), dma, dma,
        ],
        compiler_params=pltpu.CompilerParams(
            collective_id=0, has_side_effects=True, vmem_limit_bytes=48 << 20
        ),
        name="attend_all",
    )(
        queries, new_token_keys, new_token_values,
        cache_keys.reshape(blocks, KROWS, D), cache_values.reshape(blocks, KROWS, D), table,
    )


def solution(mesh):
    return jax.shard_map(
        body,
        mesh=mesh,
        in_specs=(
            P(("seq", "ctx"), None),
            P(("seq", "ctx"), None),
            P(("seq", "ctx"), None),
            P("seq", "ctx", None),
            P("seq", "ctx", None),
            P("seq", None, "ctx", None),
            P("seq", None, "ctx"),
        ),
        out_specs=P(("seq", "ctx"), None),
        check_vma=False,
    )
```

```python
import math

import jax
import jax.numpy as jnp
from jax import lax
from jax.experimental import pallas as pl
from jax.experimental.pallas import tpu as pltpu
from jax.sharding import PartitionSpec as P

HEADS = 8
ROWS = 64
KROWS = 128
KQ = 12
D = 128
NB = 8
BLOCKS = 64
CTX = 4
ZS = 8
PIECE = ROWS // CTX
WIDE = HEADS * D
MSG = WIDE + D
LAG = 2
C = math.log2(math.e) / math.sqrt(D)
NT = (((1,), (1,)), ((), ()))
MESH = pl.DeviceIdType.MESH
F32, BF16 = jnp.float32, jnp.bfloat16


def member(z, group):
    near_z = jnp.minimum(z, ZS - 1 - z)
    return 2 * jnp.where(group % 2 == 0, near_z, 3 - near_z) + jnp.where(z >= 4, 1, 0)


def z_of(e, group):
    near_z = jnp.where(group % 2 == 0, e // 2, 3 - e // 2)
    return jnp.where(e % 2 == 0, near_z, ZS - 1 - near_z)


def kernel(
    q_hbm, nk_hbm, nv_hbm, k_hbm, v_hbm, ids_hbm, used_hbm, out_hbm,
    q_buf, k_buf, v_buf, nks, nvs, kvs, kvn, ids, used, own_tbl, tbl_buf, tbl, s_buf, acc, lse, nacc, nlse, msg, rcv, fin,
    load_sem, q_send, q_recv, y_send, y_recv, kv_send, kv_recv, t_send, t_recv, m_send, m_recv, f_send, f_recv, smem_sem,
):
    s, c = lax.axis_index("seq"), lax.axis_index("ctx")
    x, z, core = s // 16, (s // 2) % ZS, s % 2
    group, e = s // HEADS, s % HEADS
    zt = z_of(e, group)
    mine = x * 2 + core

    def f_seq(n):
        return ((n // 2) * ZS + zt) * 2 + n % 2

    loads = [
        pltpu.make_async_copy(nk_hbm, nks, load_sem.at[0]),
        pltpu.make_async_copy(nv_hbm, nvs, load_sem.at[1]),
        pltpu.make_async_copy(k_hbm, k_buf, load_sem.at[2]),
        pltpu.make_async_copy(v_hbm, v_buf, load_sem.at[3]),
        pltpu.make_async_copy(ids_hbm, ids, load_sem.at[4]),
        pltpu.make_async_copy(used_hbm, used, load_sem.at[5]),
    ]
    for load in loads:
        load.start()

    def signal(seq, ctx):
        pl.semaphore_signal(barrier, inc=1, device_id=(seq, ctx), device_id_type=MESH)

    barrier = pltpu.get_barrier_semaphore()
    expected = jnp.int32(7 + 3)
    for j in range(1, CTX):
        signal(s, (c + j) % CTX)
    for j in range(1, HEADS):
        signal(group * HEADS + (e + j) % HEADS, c)
    for n in range(NB):
        seq = ((n // 2) * ZS + zt) * 2 + n % 2
        pl.when(seq != s)(lambda seq=seq: signal(seq, c))
    near_b = c * ZS + zt
    for role in range(2):
        for i in range(8):
            seq, ctx = (near_b - role) * 2 + i % 2, i // 2
            ok = (near_b - role >= 0) & ((seq != s) | (ctx != c))
            pl.when(ok)(lambda seq=seq, ctx=ctx: signal(seq, ctx))

    def q_dest(g):
        return g * HEADS + member(z, g)

    def kv_dest(role, g):
        b = x * ZS + z + role
        return g * HEADS + member(b % ZS, g), b // ZS

    for g in range(8):
        expected += jnp.where(q_dest(g) != s, 1, 0)
        for role in range(2):
            seq, ctx = kv_dest(role, g)
            expected += jnp.where((ctx < CTX) & ((seq != s) | (ctx != c)), 1, 0)

    for i in (0, 1, 4, 5):
        loads[i].wait()
    own_tbl[...] = jnp.zeros_like(own_tbl)
    for t in range(KQ):
        own_tbl[t:t + 1, :BLOCKS] = jnp.where(t < used[0], ids[t], ids[0])
    own_tbl[KQ:KQ + 1, :BLOCKS] = used[0]
    for g in range(8):
        kvs[g, :, :D] = nks[:, g * D:(g + 1) * D]
        kvs[g, :, D:] = nvs[:, g * D:(g + 1) * D]

    @pl.when(near_b == 0)
    def _():
        kvn[:KROWS] = jnp.zeros((KROWS, 2 * D), BF16)

    pl.semaphore_wait(barrier, expected)

    def remote(src, dst, send, recv, seq, ctx):
        return pltpu.make_async_remote_copy(
            src_ref=src, dst_ref=dst, send_sem=send, recv_sem=recv, device_id=(seq, ctx), device_id_type=MESH
        )

    def t_copy(j):
        to = (e + j) % HEADS
        return remote(own_tbl, tbl_buf.at[e], t_send.at[j], t_recv, group * HEADS + to, c)

    t_own = pltpu.make_async_copy(own_tbl, tbl_buf.at[e], t_recv)
    t_own.start()
    for j in range(1, HEADS):
        t_copy(j).start()

    rows_c = pl.ds(pl.multiple_of(c * PIECE, PIECE), PIECE)

    def q_copy(g):
        src, dst = q_hbm.at[:, pl.ds(g * WIDE, WIDE)], q_buf.at[mine, rows_c]
        return (
            remote(src, dst, q_send.at[g], q_recv.at[mine], q_dest(g), c),
            pltpu.make_async_copy(src, dst, q_recv.at[mine]),
        )

    def start_either(copies, own):
        pl.when(own)(copies[1].start)
        pl.when(jnp.logical_not(own))(copies[0].start)

    for g in range(8):
        start_either(q_copy(g), q_dest(g) == s)

    def kv_copy(role, g):
        seq, ctx = kv_dest(role, g)
        row = (1 - role) * KROWS + core * ROWS + c * PIECE
        dst = kvn.at[pl.ds(pl.multiple_of(row, PIECE), PIECE)]
        own = (seq == s) & (ctx == c)
        return (
            remote(kvs.at[g], dst, kv_send.at[role * 8 + g], kv_recv, seq, ctx),
            pltpu.make_async_copy(kvs.at[g], dst, kv_recv),
            own,
            (ctx < CTX) & jnp.logical_not(own),
        )

    for role in range(2):
        for g in range(8):
            there, here, own, other = kv_copy(role, g)
            pl.when(own)(here.start)
            pl.when(other)(there.start)

    def landed(ref, sem):
        pltpu.make_async_copy(ref, ref, sem).wait()

    def y_copy(n, j):
        piece = q_buf.at[n, rows_c]
        return remote(piece, piece, y_send.at[j - 1, n], y_recv.at[j - 1, n], s, (c + j) % CTX)

    def forward(n, _):
        landed(q_buf.at[n, rows_c], q_recv.at[n])
        for j in range(1, CTX):
            y_copy(n, j).start()
        return 0

    lax.fori_loop(0, NB, forward, 0)

    landed(tbl_buf, t_recv)
    to_smem = pltpu.make_async_copy(tbl_buf, tbl, smem_sem)
    to_smem.start()
    loads[2].wait()
    loads[3].wait()
    to_smem.wait()

    lane = lax.broadcasted_iota(jnp.int32, (1, D), 1)

    def finish(o, l, m, h, o_ref, total):
        o_ref[:, h * D:(h + 1) * D] = o * (1.0 / l)
        return jnp.where(lane % HEADS == h, m + jnp.log2(l), total)

    def near(n):
        @pl.when(n % 2 == 0)
        def _():
            pl.when(near_b > 0)(lambda: landed(kvn, kv_recv))
            pl.when(near_b == 0)(lambda: landed(kvn.at[pl.ds(KROWS, KROWS)], kv_recv))

        key = lax.broadcasted_iota(jnp.int32, (ROWS, 2 * KROWS), 1)
        row = lax.broadcasted_iota(jnp.int32, (ROWS, 2 * KROWS), 0)
        first = jnp.where(near_b > 0, 0, KROWS)
        visible = (key >= first) & (key <= row + (KROWS + (n % 2) * ROWS))
        total = jnp.zeros((ROWS, D), F32)
        for h in range(HEADS):
            sc = lax.dot_general(q_buf[n, :, h * D:(h + 1) * D], kvn[:, :D], NT, preferred_element_type=F32)
            sc = jnp.where(visible, sc * C, -jnp.inf)
            m = jnp.max(sc, axis=1, keepdims=True)
            p = jnp.exp2(sc - m)
            l = jnp.sum(p, axis=1, keepdims=True)
            o = jnp.dot(p.astype(BF16), kvn[:, D:], preferred_element_type=F32)
            total = finish(o, l, m, h, nacc, total)
        nlse[...] = total

    def attend(n):
        block = f_seq(n)
        tops = []
        for h in range(HEADS):
            qq = q_buf[n, :, h * D:(h + 1) * D]
            m = jnp.full((ROWS, KROWS), -jnp.inf, F32)
            for t in range(0, KQ, 2):
                kk = jnp.concatenate([k_buf[tbl[h, t + i, block]] for i in range(2)], 0)
                sc = lax.dot_general(qq, kk, NT, preferred_element_type=F32)
                s_buf[h, :, t * KROWS:(t + 2) * KROWS] = sc
                m = jnp.maximum(m, jnp.maximum(sc[:, :KROWS], sc[:, KROWS:]))
            tops.append(jnp.max(m, axis=1, keepdims=True) * C)
        total = jnp.zeros((ROWS, D), F32)
        for h in range(HEADS):
            count, m = tbl[h, KQ, block], tops[h]
            o = jnp.zeros((ROWS, D), F32)
            l = jnp.zeros((ROWS, KROWS), F32)
            for t in range(0, KQ, 2):
                parts = []
                for i in range(2):
                    shift = m + jnp.where(t + i < count, 0.0, jnp.inf)
                    p = jnp.exp2(s_buf[h, :, (t + i) * KROWS:(t + i + 1) * KROWS] * C - shift)
                    l = l + p
                    parts.append(p.astype(BF16))
                vv = jnp.concatenate([v_buf[tbl[h, t + i, block]] for i in range(2)], 0)
                o = o + jnp.dot(jnp.concatenate(parts, 1), vv, preferred_element_type=F32)
            total = finish(o, jnp.sum(l, axis=1, keepdims=True), m, h, acc, total)
        lse[...] = total

    def merge_near():
        top = jnp.maximum(lse[...], nlse[...])
        w0, w1 = jnp.exp2(lse[...] - top), jnp.exp2(nlse[...] - top)
        both = w0 + w1
        w0, w1 = w0 / both, w1 / both
        for h in range(HEADS):
            cols = slice(h * D, (h + 1) * D)
            acc[:, cols] = acc[:, cols] * w0[:, h:h + 1] + nacc[:, cols] * w1[:, h:h + 1]
        lse[...] = top + jnp.log2(both)

    def pack(n):
        for h in range(HEADS):
            msg[n, :, h * D:(h + 1) * D] = acc[:, h * D:(h + 1) * D].astype(BF16)
        full = lse[...]
        one = full.astype(BF16)
        rest = full - one.astype(F32)
        two = rest.astype(BF16)
        three = (rest - two.astype(F32)).astype(BF16)
        terms = jnp.where(lane < HEADS, one.astype(F32), jnp.where(lane < 2 * HEADS, two.astype(F32), three.astype(F32)))
        msg[n, :, WIDE:] = terms.astype(BF16)

    def m_copy(n, j):
        to = (c + j) % CTX
        src = msg.at[n, pl.ds(pl.multiple_of(to * PIECE, PIECE), PIECE)]
        return remote(src, rcv.at[j - 1, n], m_send.at[j - 1, n], m_recv.at[j - 1, n], s, to)

    def f_copy(n):
        dst = out_hbm.at[:, pl.ds(pl.multiple_of(group * WIDE, WIDE), WIDE)]
        return (
            remote(fin.at[n], dst, f_send.at[n], f_recv, f_seq(n), c),
            pltpu.make_async_copy(fin.at[n], dst, f_recv),
        )

    def join(n):
        for j in range(1, CTX):
            landed(rcv.at[j - 1, n], m_recv.at[j - 1, n])
        parts = [msg.at[n, rows_c]] + [rcv.at[j, n] for j in range(CTX - 1)]
        logs = []
        for part in parts:
            terms = part[:, WIDE:].astype(F32)
            logs.append(terms + pltpu.roll(terms, D - HEADS, 1) + pltpu.roll(terms, D - 2 * HEADS, 1))
        top = jnp.maximum(jnp.maximum(logs[0], logs[1]), jnp.maximum(logs[2], logs[3]))
        weights = [jnp.exp2(log - top) for log in logs]
        inverse = 1.0 / (weights[0] + weights[1] + weights[2] + weights[3])
        weights = [w * inverse for w in weights]
        for h in range(HEADS):
            cols = slice(h * D, (h + 1) * D)
            o = sum(part[:, cols].astype(F32) * w[:, h:h + 1] for part, w in zip(parts, weights))
            fin[n, :, cols] = o.astype(BF16)
        start_either(f_copy(n), f_seq(n) == s)

    def step(n, _):
        @pl.when(n < NB)
        def _():
            for j in range(1, CTX):
                rows = pl.ds(pl.multiple_of(((c + CTX - j) % CTX) * PIECE, PIECE), PIECE)
                landed(q_buf.at[n, rows], y_recv.at[j - 1, n])
            is_near = n // 2 == c
            pl.when(is_near)(lambda: near(n))
            attend(n)
            pl.when(is_near)(merge_near)
            pack(n)
            for j in range(1, CTX):
                m_copy(n, j).start()

        pl.when(n >= LAG)(lambda: join(n - LAG))
        return 0

    lax.fori_loop(0, NB + LAG, step, 0)

    for j in range(1, HEADS):
        t_copy(j).wait_send()
    for g in range(8):
        pl.when(q_dest(g) != s)(q_copy(g)[0].wait_send)
        for role in range(2):
            there, _, _, other = kv_copy(role, g)
            pl.when(other)(there.wait_send)

    def drain(n, _):
        for j in range(1, CTX):
            y_copy(n, j).wait_send()
            m_copy(n, j).wait_send()
        pl.when(f_seq(n) != s)(f_copy(n)[0].wait_send)
        return 0

    lax.fori_loop(0, NB, drain, 0)
    landed(out_hbm, f_recv)


def body(queries, new_token_keys, new_token_values, cache_keys, cache_values, block_ids, block_counts):
    ids = block_ids[0].transpose(2, 1, 0)
    used = block_counts.transpose(0, 2, 1)
    blocks = cache_keys.shape[1] // KROWS
    hbm = pl.BlockSpec(memory_space=pl.ANY)
    dma = pltpu.SemaphoreType.DMA
    return pl.pallas_call(
        kernel,
        out_shape=jax.ShapeDtypeStruct(queries.shape, BF16),
        in_specs=[hbm] * 7,
        out_specs=hbm,
        scratch_shapes=[
            pltpu.VMEM((NB, ROWS, WIDE), BF16),
            pltpu.VMEM((blocks, KROWS, D), BF16),
            pltpu.VMEM((blocks, KROWS, D), BF16),
            pltpu.VMEM((PIECE, WIDE), BF16),
            pltpu.VMEM((PIECE, WIDE), BF16),
            pltpu.VMEM((8, PIECE, 2 * D), BF16),
            pltpu.VMEM((2 * KROWS, 2 * D), BF16),
            pltpu.VMEM(ids.shape, jnp.int32),
            pltpu.VMEM(used.shape, jnp.int32),
            pltpu.VMEM((16, D), jnp.int32),
            pltpu.VMEM((HEADS, 16, D), jnp.int32),
            pltpu.SMEM((HEADS, 16, D), jnp.int32),
            pltpu.VMEM((HEADS, ROWS, KQ * KROWS), F32),
            pltpu.VMEM((ROWS, WIDE), F32),
            pltpu.VMEM((ROWS, D), F32),
            pltpu.VMEM((ROWS, WIDE), F32),
            pltpu.VMEM((ROWS, D), F32),
            pltpu.VMEM((NB, ROWS, MSG), BF16),
            pltpu.VMEM((CTX - 1, NB, PIECE, MSG), BF16),
            pltpu.VMEM((NB, PIECE, WIDE), BF16),
            dma((6,)), dma((8,)), dma((NB,)), dma((CTX - 1, NB)), dma((CTX - 1, NB)), dma((16,)), dma, dma((HEADS,)), dma,
            dma((CTX - 1, NB)), dma((CTX - 1, NB)), dma((NB,)), dma, dma,
        ],
        compiler_params=pltpu.CompilerParams(
            collective_id=0, has_side_effects=True
        ),
        name="attend_all",
    )(
        queries, new_token_keys, new_token_values,
        cache_keys.reshape(blocks, KROWS, D), cache_values.reshape(blocks, KROWS, D), ids, used,
    )


def solution(mesh):
    return jax.shard_map(
        body,
        mesh=mesh,
        in_specs=(
            P(("seq", "ctx"), None),
            P(("seq", "ctx"), None),
            P(("seq", "ctx"), None),
            P("seq", "ctx", None),
            P("seq", "ctx", None),
            P("seq", None, "ctx", None),
            P("seq", None, "ctx"),
        ),
        out_specs=P(("seq", "ctx"), None),
        check_vma=False,
    )
```

```python
import math

import jax
import jax.numpy as jnp
from jax import lax
from jax.experimental import pallas as pl
from jax.experimental.pallas import tpu as pltpu
from jax.sharding import PartitionSpec as P

HEADS = 8
ROWS = 64
KROWS = 128
KQ = 12
D = 128
NB = 8
BLOCKS = 64
CTX = 4
ZS = 8
PIECE = ROWS // CTX
WIDE = HEADS * D
MSG = WIDE + D
LAG = 4
AHEAD = 3
C = math.log2(math.e) / math.sqrt(D)
NT = (((1,), (1,)), ((), ()))
MESH = pl.DeviceIdType.MESH
F32, BF16 = jnp.float32, jnp.bfloat16


def member(z, group):
    near_z = jnp.minimum(z, ZS - 1 - z)
    return 2 * jnp.where(group % 2 == 0, near_z, 3 - near_z) + jnp.where(z >= 4, 1, 0)


def z_of(e, group):
    near_z = jnp.where(group % 2 == 0, e // 2, 3 - e // 2)
    return jnp.where(e % 2 == 0, near_z, ZS - 1 - near_z)


def kernel(
    q_hbm, nk_hbm, nv_hbm, k_hbm, v_hbm, ids_hbm, used_hbm, out_hbm,
    q_buf, k_buf, v_buf, nks, nvs, kvs, kvn, ids, used, own_tbl, tbl_buf, tbl, s_buf, acc, lse, nacc, nlse, msg, rcv, fin,
    load_sem, q_send, q_recv, y_send, y_recv, kv_send, kv_recv, t_send, t_recv, m_send, m_recv, f_send, f_recv, smem_sem,
):
    s, c = lax.axis_index("seq"), lax.axis_index("ctx")
    x, z, core = s // 16, (s // 2) % ZS, s % 2
    group, e = s // HEADS, s % HEADS
    zt = z_of(e, group)
    mine = x * 2 + core

    def f_seq(n):
        return ((n // 2) * ZS + zt) * 2 + n % 2

    loads = [
        pltpu.make_async_copy(nk_hbm, nks, load_sem.at[0]),
        pltpu.make_async_copy(nv_hbm, nvs, load_sem.at[1]),
        pltpu.make_async_copy(k_hbm, k_buf, load_sem.at[2]),
        pltpu.make_async_copy(v_hbm, v_buf, load_sem.at[3]),
        pltpu.make_async_copy(ids_hbm, ids, load_sem.at[4]),
        pltpu.make_async_copy(used_hbm, used, load_sem.at[5]),
    ]
    for load in loads:
        load.start()

    def signal(seq, ctx):
        pl.semaphore_signal(barrier, inc=1, device_id=(seq, ctx), device_id_type=MESH)

    barrier = pltpu.get_barrier_semaphore()
    expected = jnp.int32(7 + 3)
    for j in range(1, CTX):
        signal(s, (c + j) % CTX)
    for j in range(1, HEADS):
        signal(group * HEADS + (e + j) % HEADS, c)
    for n in range(NB):
        seq = ((n // 2) * ZS + zt) * 2 + n % 2
        pl.when(seq != s)(lambda seq=seq: signal(seq, c))
    near_b = c * ZS + zt
    for role in range(2):
        for i in range(8):
            seq, ctx = (near_b - role) * 2 + i % 2, i // 2
            ok = (near_b - role >= 0) & ((seq != s) | (ctx != c))
            pl.when(ok)(lambda seq=seq, ctx=ctx: signal(seq, ctx))

    def q_dest(g):
        return g * HEADS + member(z, g)

    def kv_dest(role, g):
        b = x * ZS + z + role
        return g * HEADS + member(b % ZS, g), b // ZS

    for g in range(8):
        expected += jnp.where(q_dest(g) != s, 1, 0)
        for role in range(2):
            seq, ctx = kv_dest(role, g)
            expected += jnp.where((ctx < CTX) & ((seq != s) | (ctx != c)), 1, 0)

    for i in (0, 1, 4, 5):
        loads[i].wait()
    own_tbl[...] = jnp.zeros_like(own_tbl)
    for t in range(KQ):
        own_tbl[t:t + 1, :BLOCKS] = jnp.where(t < used[0], ids[t], ids[0])
    own_tbl[KQ:KQ + 1, :BLOCKS] = used[0]
    for g in range(8):
        kvs[g, :, :D] = nks[:, g * D:(g + 1) * D]
        kvs[g, :, D:] = nvs[:, g * D:(g + 1) * D]

    @pl.when(near_b == 0)
    def _():
        kvn[:KROWS] = jnp.zeros((KROWS, 2 * D), BF16)

    pl.semaphore_wait(barrier, expected)

    def remote(src, dst, send, recv, seq, ctx):
        return pltpu.make_async_remote_copy(
            src_ref=src, dst_ref=dst, send_sem=send, recv_sem=recv, device_id=(seq, ctx), device_id_type=MESH
        )

    def t_copy(j):
        to = (e + j) % HEADS
        return remote(own_tbl, tbl_buf.at[e], t_send.at[j], t_recv, group * HEADS + to, c)

    t_own = pltpu.make_async_copy(own_tbl, tbl_buf.at[e], t_recv)
    t_own.start()
    for j in range(1, HEADS):
        t_copy(j).start()

    rows_c = pl.ds(pl.multiple_of(c * PIECE, PIECE), PIECE)

    def order(u):
        return (group + u) % NB

    def q_copy(t):
        g = (mine + NB - t) % NB
        src, dst = q_hbm.at[:, pl.ds(pl.multiple_of(g * WIDE, WIDE), WIDE)], q_buf.at[mine, rows_c]
        return (
            remote(src, dst, q_send.at[t], q_recv.at[mine], q_dest(g), c),
            pltpu.make_async_copy(src, dst, q_recv.at[mine]),
            q_dest(g) == s,
        )

    def start_either(there, here, own):
        pl.when(own)(here.start)
        pl.when(jnp.logical_not(own))(there.start)

    for t in range(2):
        start_either(*q_copy(t))

    def kv_copy(role, g):
        seq, ctx = kv_dest(role, g)
        row = (1 - role) * KROWS + core * ROWS + c * PIECE
        dst = kvn.at[pl.ds(pl.multiple_of(row, PIECE), PIECE)]
        own = (seq == s) & (ctx == c)
        return (
            remote(kvs.at[g], dst, kv_send.at[role * 8 + g], kv_recv, seq, ctx),
            pltpu.make_async_copy(kvs.at[g], dst, kv_recv),
            own,
            (ctx < CTX) & jnp.logical_not(own),
        )

    for role in range(2):
        for g in range(8):
            there, here, own, other = kv_copy(role, g)
            pl.when(own)(here.start)
            pl.when(other)(there.start)

    for t in range(2, NB):
        start_either(*q_copy(t))

    def landed(ref, sem):
        pltpu.make_async_copy(ref, ref, sem).wait()

    def y_copy(n, j):
        piece = q_buf.at[n, rows_c]
        return remote(piece, piece, y_send.at[j - 1, n], y_recv.at[j - 1, n], s, (c + j) % CTX)

    def forward(n):
        landed(q_buf.at[n, rows_c], q_recv.at[n])
        for j in range(1, CTX):
            y_copy(n, j).start()

    for u in range(AHEAD):
        forward(order(u))

    landed(tbl_buf, t_recv)
    to_smem = pltpu.make_async_copy(tbl_buf, tbl, smem_sem)
    to_smem.start()
    loads[2].wait()
    loads[3].wait()
    to_smem.wait()

    lane = lax.broadcasted_iota(jnp.int32, (1, D), 1)

    def finish(o, l, m, h, o_ref, total):
        o_ref[:, h * D:(h + 1) * D] = o * (1.0 / l)
        return jnp.where(lane % HEADS == h, m + jnp.log2(l), total)

    def near(n):
        @pl.when((n % 2 == 1) == (group == 2 * c + 1))
        def _():
            pl.when(near_b > 0)(lambda: landed(kvn, kv_recv))
            pl.when(near_b == 0)(lambda: landed(kvn.at[pl.ds(KROWS, KROWS)], kv_recv))

        half = HEADS // 2
        key = lax.broadcasted_iota(jnp.int32, (half * ROWS, 2 * KROWS), 1)
        row = lax.broadcasted_iota(jnp.int32, (half * ROWS, 2 * KROWS), 0) % ROWS
        first = jnp.where(near_b > 0, 0, KROWS)
        visible = (key >= first) & (key <= row + (KROWS + (n % 2) * ROWS))
        total = jnp.zeros((ROWS, D), F32)
        for h0 in (0, half):
            qq = jnp.concatenate([q_buf[n, :, h * D:(h + 1) * D] for h in range(h0, h0 + half)], 0)
            sc = lax.dot_general(qq, kvn[:, :D], NT, preferred_element_type=F32)
            sc = jnp.where(visible, sc * C, -jnp.inf)
            m = jnp.max(sc, axis=1, keepdims=True)
            p = jnp.exp2(sc - m)
            l = jnp.sum(p, axis=1, keepdims=True)
            o = jnp.dot(p.astype(BF16), kvn[:, D:], preferred_element_type=F32) * (1.0 / l)
            logs = m + jnp.log2(l)
            for h in range(h0, h0 + half):
                rows = slice((h - h0) * ROWS, (h - h0 + 1) * ROWS)
                nacc[:, h * D:(h + 1) * D] = o[rows]
                total = jnp.where(lane % HEADS == h, logs[rows], total)
        nlse[...] = total

    def attend(n):
        block = f_seq(n)
        tops = []
        for h in range(HEADS):
            qq = q_buf[n, :, h * D:(h + 1) * D]
            m = jnp.full((ROWS, KROWS), -jnp.inf, F32)
            for t in range(0, KQ, 2):
                kk = jnp.concatenate([k_buf[tbl[h, t + i, block]] for i in range(2)], 0)
                sc = lax.dot_general(qq, kk, NT, preferred_element_type=F32)
                s_buf[h, :, t * KROWS:(t + 2) * KROWS] = sc
                m = jnp.maximum(m, jnp.maximum(sc[:, :KROWS], sc[:, KROWS:]))
            tops.append(jnp.max(m, axis=1, keepdims=True) * C)
        total = jnp.zeros((ROWS, D), F32)
        for h in range(HEADS):
            count, m = tbl[h, KQ, block], tops[h]
            o = jnp.zeros((ROWS, D), F32)
            l = jnp.zeros((ROWS, KROWS), F32)
            for t in range(0, KQ, 2):
                parts = []
                for i in range(2):
                    shift = m + jnp.where(t + i < count, 0.0, jnp.inf)
                    p = jnp.exp2(s_buf[h, :, (t + i) * KROWS:(t + i + 1) * KROWS] * C - shift)
                    l = l + p
                    parts.append(p.astype(BF16))
                vv = jnp.concatenate([v_buf[tbl[h, t + i, block]] for i in range(2)], 0)
                o = o + jnp.dot(jnp.concatenate(parts, 1), vv, preferred_element_type=F32)
            total = finish(o, jnp.sum(l, axis=1, keepdims=True), m, h, acc, total)
        lse[...] = total

    def merge_near():
        top = jnp.maximum(lse[...], nlse[...])
        w0, w1 = jnp.exp2(lse[...] - top), jnp.exp2(nlse[...] - top)
        both = w0 + w1
        w0, w1 = w0 / both, w1 / both
        for h in range(HEADS):
            cols = slice(h * D, (h + 1) * D)
            acc[:, cols] = acc[:, cols] * w0[:, h:h + 1] + nacc[:, cols] * w1[:, h:h + 1]
        lse[...] = top + jnp.log2(both)

    def pack(n):
        for h in range(HEADS):
            msg[n, :, h * D:(h + 1) * D] = acc[:, h * D:(h + 1) * D].astype(BF16)
        full = lse[...]
        one = full.astype(BF16)
        rest = full - one.astype(F32)
        two = rest.astype(BF16)
        three = (rest - two.astype(F32)).astype(BF16)
        terms = jnp.where(lane < HEADS, one.astype(F32), jnp.where(lane < 2 * HEADS, two.astype(F32), three.astype(F32)))
        msg[n, :, WIDE:] = terms.astype(BF16)

    def m_copy(n, j):
        to = (c + j) % CTX
        src = msg.at[n, pl.ds(pl.multiple_of(to * PIECE, PIECE), PIECE)]
        return remote(src, rcv.at[j - 1, n], m_send.at[j - 1, n], m_recv.at[j - 1, n], s, to)

    def f_copy(n):
        dst = out_hbm.at[:, pl.ds(pl.multiple_of(group * WIDE, WIDE), WIDE)]
        return (
            remote(fin.at[n], dst, f_send.at[n], f_recv, f_seq(n), c),
            pltpu.make_async_copy(fin.at[n], dst, f_recv),
        )

    def join(n):
        for j in range(1, CTX):
            landed(rcv.at[j - 1, n], m_recv.at[j - 1, n])
        parts = [msg.at[n, rows_c]] + [rcv.at[j, n] for j in range(CTX - 1)]
        logs = []
        for part in parts:
            terms = part[:, WIDE:].astype(F32)
            logs.append(terms + pltpu.roll(terms, D - HEADS, 1) + pltpu.roll(terms, D - 2 * HEADS, 1))
        top = jnp.maximum(jnp.maximum(logs[0], logs[1]), jnp.maximum(logs[2], logs[3]))
        weights = [jnp.exp2(log - top) for log in logs]
        inverse = 1.0 / (weights[0] + weights[1] + weights[2] + weights[3])
        weights = [w * inverse for w in weights]
        for h in range(HEADS):
            cols = slice(h * D, (h + 1) * D)
            o = sum(part[:, cols].astype(F32) * w[:, h:h + 1] for part, w in zip(parts, weights))
            fin[n, :, cols] = o.astype(BF16)
        start_either(*f_copy(n), f_seq(n) == s)

    def step(u, _):
        pl.when(u < NB - AHEAD)(lambda: forward(order(u + AHEAD)))

        @pl.when(u < NB)
        def _():
            n = order(u)
            for j in range(1, CTX):
                rows = pl.ds(pl.multiple_of(((c + CTX - j) % CTX) * PIECE, PIECE), PIECE)
                landed(q_buf.at[n, rows], y_recv.at[j - 1, n])
            is_near = n // 2 == c
            pl.when(is_near)(lambda: near(n))
            attend(n)
            pl.when(is_near)(merge_near)
            pack(n)
            for j in range(1, CTX):
                m_copy(n, j).start()

        pl.when(u >= LAG)(lambda: join(order(u - LAG)))
        return 0

    lax.fori_loop(0, NB + LAG, step, 0)

    for j in range(1, HEADS):
        t_copy(j).wait_send()
    for g in range(8):
        there, _, own = q_copy(g)
        pl.when(jnp.logical_not(own))(there.wait_send)
        for role in range(2):
            there, _, _, other = kv_copy(role, g)
            pl.when(other)(there.wait_send)

    def drain(n, _):
        for j in range(1, CTX):
            y_copy(n, j).wait_send()
            m_copy(n, j).wait_send()
        pl.when(f_seq(n) != s)(f_copy(n)[0].wait_send)
        return 0

    lax.fori_loop(0, NB, drain, 0)
    landed(out_hbm, f_recv)


def body(queries, new_token_keys, new_token_values, cache_keys, cache_values, block_ids, block_counts):
    ids = block_ids[0].transpose(2, 1, 0)
    used = block_counts.transpose(0, 2, 1)
    blocks = cache_keys.shape[1] // KROWS
    hbm = pl.BlockSpec(memory_space=pltpu.MemorySpace.HBM)
    dma = pltpu.SemaphoreType.DMA
    return pl.pallas_call(
        kernel,
        out_shape=jax.ShapeDtypeStruct(queries.shape, BF16),
        in_specs=[hbm] * 7,
        out_specs=pl.BlockSpec(memory_space=pl.ANY),
        scratch_shapes=[
            pltpu.VMEM((NB, ROWS, WIDE), BF16),
            pltpu.VMEM((blocks, KROWS, D), BF16),
            pltpu.VMEM((blocks, KROWS, D), BF16),
            pltpu.VMEM((PIECE, WIDE), BF16),
            pltpu.VMEM((PIECE, WIDE), BF16),
            pltpu.VMEM((8, PIECE, 2 * D), BF16),
            pltpu.VMEM((2 * KROWS, 2 * D), BF16),
            pltpu.VMEM(ids.shape, jnp.int32),
            pltpu.VMEM(used.shape, jnp.int32),
            pltpu.VMEM((16, D), jnp.int32),
            pltpu.VMEM((HEADS, 16, D), jnp.int32),
            pltpu.SMEM((HEADS, 16, D), jnp.int32),
            pltpu.VMEM((HEADS, ROWS, KQ * KROWS), F32),
            pltpu.VMEM((ROWS, WIDE), F32),
            pltpu.VMEM((ROWS, D), F32),
            pltpu.VMEM((ROWS, WIDE), F32),
            pltpu.VMEM((ROWS, D), F32),
            pltpu.VMEM((NB, ROWS, MSG), BF16),
            pltpu.VMEM((CTX - 1, NB, PIECE, MSG), BF16),
            pltpu.VMEM((NB, PIECE, WIDE), BF16),
            dma((6,)), dma((8,)), dma((NB,)), dma((CTX - 1, NB)), dma((CTX - 1, NB)), dma((16,)), dma, dma((HEADS,)), dma,
            dma((CTX - 1, NB)), dma((CTX - 1, NB)), dma((NB,)), dma, dma,
        ],
        compiler_params=pltpu.CompilerParams(
            collective_id=0, has_side_effects=True
        ),
        name="attend_all",
    )(
        queries, new_token_keys, new_token_values,
        cache_keys.reshape(blocks, KROWS, D), cache_values.reshape(blocks, KROWS, D), ids, used,
    )


def solution(mesh):
    return jax.shard_map(
        body,
        mesh=mesh,
        in_specs=(
            P(("seq", "ctx"), None),
            P(("seq", "ctx"), None),
            P(("seq", "ctx"), None),
            P("seq", "ctx", None),
            P("seq", "ctx", None),
            P("seq", None, "ctx", None),
            P("seq", None, "ctx"),
        ),
        out_specs=P(("seq", "ctx"), None),
        check_vma=False,
    )
```

```python
import math

import jax
import jax.numpy as jnp
from jax import lax
from jax.experimental import pallas as pl
from jax.experimental.pallas import tpu as pltpu
from jax.sharding import PartitionSpec as P

HEADS = 8
ROWS = 64
KROWS = 128
KQ = 12
D = 128
NB = 8
BLOCKS = 64
CTX = 4
ZS = 8
PIECE = ROWS // CTX
WIDE = HEADS * D
MSG = WIDE + D
LAG = 5
NEAR_AT = 3
AHEAD = 3
C = math.log2(math.e) / math.sqrt(D)
NT = (((1,), (1,)), ((), ()))
MESH = pl.DeviceIdType.MESH
F32, BF16 = jnp.float32, jnp.bfloat16


def member(z, group):
    near_z = jnp.minimum(z, ZS - 1 - z)
    return 2 * jnp.where(group % 2 == 0, near_z, 3 - near_z) + jnp.where(z >= 4, 1, 0)


def z_of(e, group):
    near_z = jnp.where(group % 2 == 0, e // 2, 3 - e // 2)
    return jnp.where(e % 2 == 0, near_z, ZS - 1 - near_z)


def kernel(
    q_hbm, nk_hbm, nv_hbm, k_hbm, v_hbm, ids_hbm, used_hbm, out_hbm,
    q_buf, k_buf, v_buf, nks, nvs, kvs, kvn, ids, used, own_tbl, tbl_buf, tbl, s_buf, acc, lse, kept, kept_lse, nacc, nlse, msg, rcv, fin,
    load_sem, q_send, q_recv, y_send, y_recv, kv_send, kv_recv, t_send, t_recv, m_send, m_recv, f_send, f_recv, smem_sem,
):
    s, c = lax.axis_index("seq"), lax.axis_index("ctx")
    x, z, core = s // 16, (s // 2) % ZS, s % 2
    group, e = s // HEADS, s % HEADS
    zt = z_of(e, group)
    mine = x * 2 + core

    def f_seq(n):
        return ((n // 2) * ZS + zt) * 2 + n % 2

    loads = [
        pltpu.make_async_copy(nk_hbm, nks, load_sem.at[0]),
        pltpu.make_async_copy(nv_hbm, nvs, load_sem.at[1]),
        pltpu.make_async_copy(k_hbm, k_buf, load_sem.at[2]),
        pltpu.make_async_copy(v_hbm, v_buf, load_sem.at[3]),
        pltpu.make_async_copy(ids_hbm, ids, load_sem.at[4]),
        pltpu.make_async_copy(used_hbm, used, load_sem.at[5]),
    ]
    for load in loads:
        load.start()

    def signal(seq, ctx):
        pl.semaphore_signal(barrier, inc=1, device_id=(seq, ctx), device_id_type=MESH)

    barrier = pltpu.get_barrier_semaphore()
    expected = jnp.int32(7 + 3)
    for j in range(1, CTX):
        signal(s, (c + j) % CTX)
    for j in range(1, HEADS):
        signal(group * HEADS + (e + j) % HEADS, c)
    for n in range(NB):
        seq = ((n // 2) * ZS + zt) * 2 + n % 2
        pl.when(seq != s)(lambda seq=seq: signal(seq, c))
    near_b = c * ZS + zt
    for role in range(2):
        for i in range(8):
            seq, ctx = (near_b - role) * 2 + i % 2, i // 2
            ok = (near_b - role >= 0) & ((seq != s) | (ctx != c))
            pl.when(ok)(lambda seq=seq, ctx=ctx: signal(seq, ctx))

    def q_dest(g):
        return g * HEADS + member(z, g)

    def kv_dest(role, g):
        b = x * ZS + z + role
        return g * HEADS + member(b % ZS, g), b // ZS

    for g in range(8):
        expected += jnp.where(q_dest(g) != s, 1, 0)
        for role in range(2):
            seq, ctx = kv_dest(role, g)
            expected += jnp.where((ctx < CTX) & ((seq != s) | (ctx != c)), 1, 0)

    for i in (0, 1, 4, 5):
        loads[i].wait()
    own_tbl[...] = jnp.zeros_like(own_tbl)
    for t in range(KQ):
        at = BLOCKS * (t // 8)
        own_tbl[t % 8:t % 8 + 1, at:at + BLOCKS] = jnp.where(t < used[0], ids[t], ids[0])
    own_tbl[KQ % 8:KQ % 8 + 1, BLOCKS:] = used[0]
    for g in range(8):
        kvs[g, :, :D] = nks[:, g * D:(g + 1) * D]
        kvs[g, :, D:] = nvs[:, g * D:(g + 1) * D]

    @pl.when(near_b == 0)
    def _():
        kvn[:KROWS] = jnp.zeros((KROWS, 2 * D), BF16)

    pl.semaphore_wait(barrier, expected)

    def remote(src, dst, send, recv, seq, ctx):
        return pltpu.make_async_remote_copy(
            src_ref=src, dst_ref=dst, send_sem=send, recv_sem=recv, device_id=(seq, ctx), device_id_type=MESH
        )

    def t_copy(j):
        to = (e + j) % HEADS
        return remote(own_tbl, tbl_buf.at[e], t_send.at[j], t_recv, group * HEADS + to, c)

    t_own = pltpu.make_async_copy(own_tbl, tbl_buf.at[e], t_recv)
    t_own.start()
    for j in range(1, HEADS):
        t_copy(j).start()

    rows_c = pl.ds(pl.multiple_of(c * PIECE, PIECE), PIECE)

    def order(u):
        return (group + u) % NB

    def q_copy(t):
        g = (mine + NB - t) % NB
        src, dst = q_hbm.at[:, pl.ds(pl.multiple_of(g * WIDE, WIDE), WIDE)], q_buf.at[mine, rows_c]
        return (
            remote(src, dst, q_send.at[t], q_recv.at[mine], q_dest(g), c),
            pltpu.make_async_copy(src, dst, q_recv.at[mine]),
            q_dest(g) == s,
        )

    def start_either(there, here, own):
        pl.when(own)(here.start)
        pl.when(jnp.logical_not(own))(there.start)

    for t in range(2):
        start_either(*q_copy(t))

    def kv_copy(role, g):
        seq, ctx = kv_dest(role, g)
        row = (1 - role) * KROWS + core * ROWS + c * PIECE
        dst = kvn.at[pl.ds(pl.multiple_of(row, PIECE), PIECE)]
        own = (seq == s) & (ctx == c)
        return (
            remote(kvs.at[g], dst, kv_send.at[role * 8 + g], kv_recv, seq, ctx),
            pltpu.make_async_copy(kvs.at[g], dst, kv_recv),
            own,
            (ctx < CTX) & jnp.logical_not(own),
        )

    for role in range(2):
        for g in range(8):
            there, here, own, other = kv_copy(role, g)
            pl.when(own)(here.start)
            pl.when(other)(there.start)

    for t in range(2, NB):
        start_either(*q_copy(t))

    def landed(ref, sem):
        pltpu.make_async_copy(ref, ref, sem).wait()

    def y_copy(n, j):
        piece = q_buf.at[n, rows_c]
        return remote(piece, piece, y_send.at[j - 1, n], y_recv.at[j - 1, n], s, (c + j) % CTX)

    def forward(n):
        landed(q_buf.at[n, rows_c], q_recv.at[n])
        for j in range(1, CTX):
            y_copy(n, j).start()

    for u in range(AHEAD):
        forward(order(u))

    landed(tbl_buf, t_recv)
    to_smem = pltpu.make_async_copy(tbl_buf, tbl, smem_sem)
    to_smem.start()
    loads[2].wait()
    loads[3].wait()
    to_smem.wait()

    lane = lax.broadcasted_iota(jnp.int32, (1, D), 1)

    def finish(o, l, m, h, o_ref, total):
        o_ref[:, h * D:(h + 1) * D] = o * (1.0 / l)
        return jnp.where(lane % HEADS == h, m + jnp.log2(l), total)

    def near(n):
        half = HEADS // 2
        key = lax.broadcasted_iota(jnp.int32, (half * ROWS, 2 * KROWS), 1)
        row = lax.broadcasted_iota(jnp.int32, (half * ROWS, 2 * KROWS), 0) % ROWS
        first = jnp.where(near_b > 0, 0, KROWS)
        visible = (key >= first) & (key <= row + (KROWS + (n % 2) * ROWS))
        total = jnp.zeros((ROWS, D), F32)
        for h0 in (0, half):
            qq = jnp.concatenate([q_buf[n, :, h * D:(h + 1) * D] for h in range(h0, h0 + half)], 0)
            sc = lax.dot_general(qq, kvn[:, :D], NT, preferred_element_type=F32)
            sc = jnp.where(visible, sc * C, -jnp.inf)
            m = jnp.max(sc, axis=1, keepdims=True)
            p = jnp.exp2(sc - m)
            l = jnp.sum(p, axis=1, keepdims=True)
            o = jnp.dot(p.astype(BF16), kvn[:, D:], preferred_element_type=F32) * (1.0 / l)
            logs = m + jnp.log2(l)
            for h in range(h0, h0 + half):
                rows = slice((h - h0) * ROWS, (h - h0 + 1) * ROWS)
                nacc[:, h * D:(h + 1) * D] = o[rows]
                total = jnp.where(lane % HEADS == h, logs[rows], total)
        nlse[...] = total

    def attend(n):
        block = f_seq(n)
        tops = []
        for h in range(HEADS):
            qq = q_buf[n, :, h * D:(h + 1) * D]
            m = jnp.full((ROWS, KROWS), -jnp.inf, F32)
            for t in range(0, KQ, 2):
                kk = jnp.concatenate([k_buf[tbl[h, (t + i) % 8, block + BLOCKS * ((t + i) // 8)]] for i in range(2)], 0)
                sc = lax.dot_general(qq, kk, NT, preferred_element_type=F32)
                s_buf[h, :, t * KROWS:(t + 2) * KROWS] = sc
                m = jnp.maximum(m, jnp.maximum(sc[:, :KROWS], sc[:, KROWS:]))
            tops.append(jnp.max(m, axis=1, keepdims=True) * C)
        total = jnp.zeros((ROWS, D), F32)
        for h in range(HEADS):
            count, m = tbl[h, KQ % 8, block + BLOCKS], tops[h]
            o = jnp.zeros((ROWS, D), F32)
            l = jnp.zeros((ROWS, KROWS), F32)
            for t in range(0, KQ, 2):
                parts = []
                for i in range(2):
                    shift = m + jnp.where(t + i < count, 0.0, jnp.inf)
                    p = jnp.exp2(s_buf[h, :, (t + i) * KROWS:(t + i + 1) * KROWS] * C - shift)
                    l = l + p
                    parts.append(p.astype(BF16))
                vv = jnp.concatenate([v_buf[tbl[h, (t + i) % 8, block + BLOCKS * ((t + i) // 8)]] for i in range(2)], 0)
                o = o + jnp.dot(jnp.concatenate(parts, 1), vv, preferred_element_type=F32)
            total = finish(o, jnp.sum(l, axis=1, keepdims=True), m, h, acc, total)
        lse[...] = total

    def merge_near():
        top = jnp.maximum(lse[...], nlse[...])
        w0, w1 = jnp.exp2(lse[...] - top), jnp.exp2(nlse[...] - top)
        both = w0 + w1
        w0, w1 = w0 / both, w1 / both
        for h in range(HEADS):
            cols = slice(h * D, (h + 1) * D)
            acc[:, cols] = acc[:, cols] * w0[:, h:h + 1] + nacc[:, cols] * w1[:, h:h + 1]
        lse[...] = top + jnp.log2(both)

    def pack(n):
        for h in range(HEADS):
            msg[n, :, h * D:(h + 1) * D] = acc[:, h * D:(h + 1) * D].astype(BF16)
        full = lse[...]
        one = full.astype(BF16)
        rest = full - one.astype(F32)
        two = rest.astype(BF16)
        three = (rest - two.astype(F32)).astype(BF16)
        terms = jnp.where(lane < HEADS, one.astype(F32), jnp.where(lane < 2 * HEADS, two.astype(F32), three.astype(F32)))
        msg[n, :, WIDE:] = terms.astype(BF16)

    def m_copy(n, j):
        to = (c + j) % CTX
        src = msg.at[n, pl.ds(pl.multiple_of(to * PIECE, PIECE), PIECE)]
        return remote(src, rcv.at[j - 1, n], m_send.at[j - 1, n], m_recv.at[j - 1, n], s, to)

    def f_copy(n):
        dst = out_hbm.at[:, pl.ds(pl.multiple_of(group * WIDE, WIDE), WIDE)]
        return (
            remote(fin.at[n], dst, f_send.at[n], f_recv, f_seq(n), c),
            pltpu.make_async_copy(fin.at[n], dst, f_recv),
        )

    def join(n):
        for j in range(1, CTX):
            landed(rcv.at[j - 1, n], m_recv.at[j - 1, n])
        parts = [msg.at[n, rows_c]] + [rcv.at[j, n] for j in range(CTX - 1)]
        logs = []
        for part in parts:
            terms = part[:, WIDE:].astype(F32)
            logs.append(terms + pltpu.roll(terms, D - HEADS, 1) + pltpu.roll(terms, D - 2 * HEADS, 1))
        top = jnp.maximum(jnp.maximum(logs[0], logs[1]), jnp.maximum(logs[2], logs[3]))
        weights = [jnp.exp2(log - top) for log in logs]
        inverse = 1.0 / (weights[0] + weights[1] + weights[2] + weights[3])
        weights = [w * inverse for w in weights]
        for h in range(HEADS):
            cols = slice(h * D, (h + 1) * D)
            o = sum(part[:, cols].astype(F32) * w[:, h:h + 1] for part, w in zip(parts, weights))
            fin[n, :, cols] = o.astype(BF16)
        start_either(*f_copy(n), f_seq(n) == s)

    def send_parts(n):
        pack(n)
        for j in (2, 1, 3):
            m_copy(n, j).start()

    def kept_near(k, _):
        n = 2 * c + k

        @pl.when((n + NB - group) % NB < NEAR_AT)
        def _():
            acc[...] = kept[k]
            lse[...] = kept_lse[k]
            near(n)
            merge_near()
            send_parts(n)

        return 0

    def step(u, _):
        @pl.when(u == NEAR_AT)
        def _():
            pl.when(near_b > 0)(lambda: landed(kvn, kv_recv))
            pl.when(near_b == 0)(lambda: landed(kvn.at[pl.ds(KROWS, KROWS)], kv_recv))
            lax.fori_loop(0, 2, kept_near, 0)

        pl.when(u < NB - AHEAD)(lambda: forward(order(u + AHEAD)))

        @pl.when(u < NB)
        def _():
            n = order(u)
            for j in range(1, CTX):
                rows = pl.ds(pl.multiple_of(((c + CTX - j) % CTX) * PIECE, PIECE), PIECE)
                landed(q_buf.at[n, rows], y_recv.at[j - 1, n])
            is_near = n // 2 == c
            later = is_near & (u < NEAR_AT)
            attend(n)

            @pl.when(later)
            def _():
                kept[n % 2] = acc[...]
                kept_lse[n % 2] = lse[...]

            @pl.when(is_near & jnp.logical_not(later))
            def _():
                near(n)
                merge_near()

            pl.when(jnp.logical_not(later))(lambda: send_parts(n))

        pl.when(u >= LAG)(lambda: join(order(u - LAG)))
        return 0

    lax.fori_loop(0, NB + LAG, step, 0)

    for j in range(1, HEADS):
        t_copy(j).wait_send()
    for g in range(8):
        there, _, own = q_copy(g)
        pl.when(jnp.logical_not(own))(there.wait_send)
        for role in range(2):
            there, _, _, other = kv_copy(role, g)
            pl.when(other)(there.wait_send)

    def drain(n, _):
        for j in range(1, CTX):
            y_copy(n, j).wait_send()
            m_copy(n, j).wait_send()
        pl.when(f_seq(n) != s)(f_copy(n)[0].wait_send)
        return 0

    lax.fori_loop(0, NB, drain, 0)
    landed(out_hbm, f_recv)


def body(queries, new_token_keys, new_token_values, cache_keys, cache_values, block_ids, block_counts):
    ids = block_ids[0].transpose(2, 1, 0)
    used = block_counts.transpose(0, 2, 1)
    blocks = cache_keys.shape[1] // KROWS
    hbm = pl.BlockSpec(memory_space=pltpu.MemorySpace.HBM)
    dma = pltpu.SemaphoreType.DMA
    return pl.pallas_call(
        kernel,
        out_shape=jax.ShapeDtypeStruct(queries.shape, BF16),
        in_specs=[hbm] * 7,
        out_specs=pl.BlockSpec(memory_space=pl.ANY),
        scratch_shapes=[
            pltpu.VMEM((NB, ROWS, WIDE), BF16),
            pltpu.VMEM((blocks, KROWS, D), BF16),
            pltpu.VMEM((blocks, KROWS, D), BF16),
            pltpu.VMEM((PIECE, WIDE), BF16),
            pltpu.VMEM((PIECE, WIDE), BF16),
            pltpu.VMEM((8, PIECE, 2 * D), BF16),
            pltpu.VMEM((2 * KROWS, 2 * D), BF16),
            pltpu.VMEM(ids.shape, jnp.int32),
            pltpu.VMEM(used.shape, jnp.int32),
            pltpu.VMEM((8, D), jnp.int32),
            pltpu.VMEM((HEADS, 8, D), jnp.int32),
            pltpu.SMEM((HEADS, 8, D), jnp.int32),
            pltpu.VMEM((HEADS, ROWS, KQ * KROWS), F32),
            pltpu.VMEM((ROWS, WIDE), F32),
            pltpu.VMEM((ROWS, D), F32),
            pltpu.VMEM((2, ROWS, WIDE), F32),
            pltpu.VMEM((2, ROWS, D), F32),
            pltpu.VMEM((ROWS, WIDE), F32),
            pltpu.VMEM((ROWS, D), F32),
            pltpu.VMEM((NB, ROWS, MSG), BF16),
            pltpu.VMEM((CTX - 1, NB, PIECE, MSG), BF16),
            pltpu.VMEM((NB, PIECE, WIDE), BF16),
            dma((6,)), dma((8,)), dma((NB,)), dma((CTX - 1, NB)), dma((CTX - 1, NB)), dma((16,)), dma, dma((HEADS,)), dma,
            dma((CTX - 1, NB)), dma((CTX - 1, NB)), dma((NB,)), dma, dma,
        ],
        compiler_params=pltpu.CompilerParams(
            collective_id=0, has_side_effects=True
        ),
        name="attend_all",
    )(
        queries, new_token_keys, new_token_values,
        cache_keys.reshape(blocks, KROWS, D), cache_values.reshape(blocks, KROWS, D), ids, used,
    )


def solution(mesh):
    return jax.shard_map(
        body,
        mesh=mesh,
        in_specs=(
            P(("seq", "ctx"), None),
            P(("seq", "ctx"), None),
            P(("seq", "ctx"), None),
            P("seq", "ctx", None),
            P("seq", "ctx", None),
            P("seq", None, "ctx", None),
            P("seq", None, "ctx"),
        ),
        out_specs=P(("seq", "ctx"), None),
        check_vma=False,
    )
```

```python
import math

import jax
import jax.numpy as jnp
from jax import lax
from jax.experimental import pallas as pl
from jax.experimental.pallas import tpu as pltpu
from jax.sharding import PartitionSpec as P

HEADS = 8
ROWS = 64
KROWS = 128
KQ = 12
D = 128
NB = 8
BLOCKS = 64
CTX = 4
ZS = 8
PIECE = ROWS // CTX
WIDE = HEADS * D
MSG = WIDE + D
LAG = 5
NEAR_AT = 3
AHEAD = 3
C = math.log2(math.e) / math.sqrt(D)
NT = (((1,), (1,)), ((), ()))
MESH = pl.DeviceIdType.MESH
F32, BF16 = jnp.float32, jnp.bfloat16


def member(z, group):
    near_z = jnp.minimum(z, ZS - 1 - z)
    return 2 * jnp.where(group % 2 == 0, near_z, 3 - near_z) + jnp.where(z >= 4, 1, 0)


def z_of(e, group):
    near_z = jnp.where(group % 2 == 0, e // 2, 3 - e // 2)
    return jnp.where(e % 2 == 0, near_z, ZS - 1 - near_z)


def kernel(
    q_hbm, nk_hbm, nv_hbm, k_hbm, v_hbm, ids_hbm, used_hbm, out_hbm,
    q_buf, k_buf, v_buf, nks, nvs, kvs, kvn, ids, used, own_tbl, tbl_buf, tbl, s_buf, acc, lse, kept, kept_lse, nacc, nlse, msg, rcv, fin,
    load_sem, q_send, q_recv, y_send, y_recv, kv_send, kv_recv, t_send, t_recv, m_send, m_recv, f_send, f_recv, smem_sem,
):
    s, c = lax.axis_index("seq"), lax.axis_index("ctx")
    x, z, core = s // 16, (s // 2) % ZS, s % 2
    group, e = s // HEADS, s % HEADS
    zt = z_of(e, group)
    mine = x * 2 + core

    def f_seq(n):
        return ((n // 2) * ZS + zt) * 2 + n % 2

    loads = [
        pltpu.make_async_copy(nk_hbm, nks, load_sem.at[0]),
        pltpu.make_async_copy(nv_hbm, nvs, load_sem.at[1]),
        pltpu.make_async_copy(k_hbm, k_buf, load_sem.at[2]),
        pltpu.make_async_copy(v_hbm, v_buf, load_sem.at[3]),
        pltpu.make_async_copy(ids_hbm, ids, load_sem.at[4]),
        pltpu.make_async_copy(used_hbm, used, load_sem.at[5]),
    ]
    for load in loads:
        load.start()

    def signal(seq, ctx):
        pl.semaphore_signal(barrier, inc=1, device_id=(seq, ctx), device_id_type=MESH)

    barrier = pltpu.get_barrier_semaphore()
    expected = jnp.int32(7 + 3)
    for j in range(1, CTX):
        signal(s, (c + j) % CTX)
    for j in range(1, HEADS):
        signal(group * HEADS + (e + j) % HEADS, c)
    for n in range(NB):
        seq = ((n // 2) * ZS + zt) * 2 + n % 2
        pl.when(seq != s)(lambda seq=seq: signal(seq, c))
    near_b = c * ZS + zt
    for role in range(2):
        for i in range(8):
            seq, ctx = (near_b - role) * 2 + i % 2, i // 2
            ok = (near_b - role >= 0) & ((seq != s) | (ctx != c))
            pl.when(ok)(lambda seq=seq, ctx=ctx: signal(seq, ctx))

    def q_dest(g):
        return g * HEADS + member(z, g)

    def kv_dest(role, g):
        b = x * ZS + z + role
        return g * HEADS + member(b % ZS, g), b // ZS

    for g in range(8):
        expected += jnp.where(q_dest(g) != s, 1, 0)
        for role in range(2):
            seq, ctx = kv_dest(role, g)
            expected += jnp.where((ctx < CTX) & ((seq != s) | (ctx != c)), 1, 0)

    for i in (0, 1, 4, 5):
        loads[i].wait()
    own_tbl[...] = jnp.zeros_like(own_tbl)
    for t in range(KQ):
        at = BLOCKS * (t // 8)
        own_tbl[t % 8:t % 8 + 1, at:at + BLOCKS] = jnp.where(t < used[0], ids[t], ids[0])
    own_tbl[KQ % 8:KQ % 8 + 1, BLOCKS:] = used[0]
    for g in range(8):
        kvs[g, :, :D] = nks[:, g * D:(g + 1) * D]
        kvs[g, :, D:] = nvs[:, g * D:(g + 1) * D]

    @pl.when(near_b == 0)
    def _():
        kvn[:KROWS] = jnp.zeros((KROWS, 2 * D), BF16)

    pl.semaphore_wait(barrier, expected)

    def remote(src, dst, send, recv, seq, ctx):
        return pltpu.make_async_remote_copy(
            src_ref=src, dst_ref=dst, send_sem=send, recv_sem=recv, device_id=(seq, ctx), device_id_type=MESH
        )

    def t_copy(j):
        to = (e + j) % HEADS
        return remote(own_tbl, tbl_buf.at[e], t_send.at[j], t_recv, group * HEADS + to, c)

    t_own = pltpu.make_async_copy(own_tbl, tbl_buf.at[e], t_recv)
    t_own.start()
    for j in range(1, HEADS):
        t_copy(j).start()

    rows_c = pl.ds(pl.multiple_of(c * PIECE, PIECE), PIECE)

    def order(u):
        return (group + u) % NB

    def q_copy(t):
        g = (mine + NB - t) % NB
        src, dst = q_hbm.at[:, pl.ds(pl.multiple_of(g * WIDE, WIDE), WIDE)], q_buf.at[mine, rows_c]
        return (
            remote(src, dst, q_send.at[t], q_recv.at[mine], q_dest(g), c),
            pltpu.make_async_copy(src, dst, q_recv.at[mine]),
            q_dest(g) == s,
        )

    def start_either(there, here, own):
        pl.when(own)(here.start)
        pl.when(jnp.logical_not(own))(there.start)

    for t in range(2):
        start_either(*q_copy(t))

    def kv_copy(role, g):
        seq, ctx = kv_dest(role, g)
        row = (1 - role) * KROWS + core * ROWS + c * PIECE
        dst = kvn.at[pl.ds(pl.multiple_of(row, PIECE), PIECE)]
        own = (seq == s) & (ctx == c)
        return (
            remote(kvs.at[g], dst, kv_send.at[role * 8 + g], kv_recv, seq, ctx),
            pltpu.make_async_copy(kvs.at[g], dst, kv_recv),
            own,
            (ctx < CTX) & jnp.logical_not(own),
        )

    for role in range(2):
        for g in range(8):
            there, here, own, other = kv_copy(role, g)
            pl.when(own)(here.start)
            pl.when(other)(there.start)

    for t in range(2, NB):
        start_either(*q_copy(t))

    def landed(ref, sem):
        pltpu.make_async_copy(ref, ref, sem).wait()

    def y_copy(n, j):
        piece = q_buf.at[n, rows_c]
        return remote(piece, piece, y_send.at[j - 1, n], y_recv.at[j - 1, n], s, (c + j) % CTX)

    def forward(n):
        landed(q_buf.at[n, rows_c], q_recv.at[n])
        for j in range(1, CTX):
            y_copy(n, j).start()

    for u in range(AHEAD):
        forward(order(u))

    landed(tbl_buf, t_recv)
    to_smem = pltpu.make_async_copy(tbl_buf, tbl, smem_sem)
    to_smem.start()
    loads[2].wait()
    loads[3].wait()
    to_smem.wait()

    lane = lax.broadcasted_iota(jnp.int32, (1, D), 1)

    def finish(o, l, m, h, o_ref, total):
        o_ref[:, h * D:(h + 1) * D] = o * (1.0 / l)
        return jnp.where(lane % HEADS == h, m + jnp.log2(l), total)

    def near(n):
        half = HEADS // 2
        key = lax.broadcasted_iota(jnp.int32, (half * ROWS, 2 * KROWS), 1)
        row = lax.broadcasted_iota(jnp.int32, (half * ROWS, 2 * KROWS), 0) % ROWS
        first = jnp.where(near_b > 0, 0, KROWS)
        visible = (key >= first) & (key <= row + (KROWS + (n % 2) * ROWS))
        total = jnp.zeros((ROWS, D), F32)
        for h0 in (0, half):
            qq = jnp.concatenate([q_buf[n, :, h * D:(h + 1) * D] for h in range(h0, h0 + half)], 0)
            sc = lax.dot_general(qq, kvn[:, :D], NT, preferred_element_type=F32)
            sc = jnp.where(visible, sc * C, -jnp.inf)
            m = jnp.max(sc, axis=1, keepdims=True)
            p = jnp.exp2(sc - m)
            l = jnp.sum(p, axis=1, keepdims=True)
            o = jnp.dot(p.astype(BF16), kvn[:, D:], preferred_element_type=F32) * (1.0 / l)
            logs = m + jnp.log2(l)
            for h in range(h0, h0 + half):
                rows = slice((h - h0) * ROWS, (h - h0 + 1) * ROWS)
                nacc[:, h * D:(h + 1) * D] = o[rows]
                total = jnp.where(lane % HEADS == h, logs[rows], total)
        nlse[...] = total

    def attend(n):
        block = f_seq(n)
        tops = []
        for h in range(HEADS):
            qq = q_buf[n, :, h * D:(h + 1) * D]
            m = jnp.full((ROWS, KROWS), -jnp.inf, F32)
            for t in range(0, KQ, 2):
                kk = jnp.concatenate([k_buf[tbl[h, (t + i) % 8, block + BLOCKS * ((t + i) // 8)]] for i in range(2)], 0)
                sc = lax.dot_general(qq, kk, NT, preferred_element_type=F32)
                s_buf[h, :, t * KROWS:(t + 2) * KROWS] = sc
                m = jnp.maximum(m, jnp.maximum(sc[:, :KROWS], sc[:, KROWS:]))
            tops.append(jnp.max(m, axis=1, keepdims=True) * C)
        total = jnp.zeros((ROWS, D), F32)
        for h in range(HEADS):
            count, m = tbl[h, KQ % 8, block + BLOCKS], tops[h]
            o = jnp.zeros((ROWS, D), F32)
            l = jnp.zeros((ROWS, KROWS), F32)
            for t in range(0, KQ, 2):
                parts = []
                for i in range(2):
                    shift = m + jnp.where(t + i < count, 0.0, jnp.inf)
                    p = jnp.exp2(s_buf[h, :, (t + i) * KROWS:(t + i + 1) * KROWS] * C - shift)
                    l = l + p
                    parts.append(p.astype(BF16))
                vv = jnp.concatenate([v_buf[tbl[h, (t + i) % 8, block + BLOCKS * ((t + i) // 8)]] for i in range(2)], 0)
                o = o + jnp.dot(jnp.concatenate(parts, 1), vv, preferred_element_type=F32)
            total = finish(o, jnp.sum(l, axis=1, keepdims=True), m, h, acc, total)
        lse[...] = total

    def merge_near():
        top = jnp.maximum(lse[...], nlse[...])
        w0, w1 = jnp.exp2(lse[...] - top), jnp.exp2(nlse[...] - top)
        both = w0 + w1
        w0, w1 = w0 / both, w1 / both
        for h in range(HEADS):
            cols = slice(h * D, (h + 1) * D)
            acc[:, cols] = acc[:, cols] * w0[:, h:h + 1] + nacc[:, cols] * w1[:, h:h + 1]
        lse[...] = top + jnp.log2(both)

    def pack(n):
        for h in range(HEADS):
            msg[n, :, h * D:(h + 1) * D] = acc[:, h * D:(h + 1) * D].astype(BF16)
        full = lse[...]
        one = full.astype(BF16)
        rest = full - one.astype(F32)
        two = rest.astype(BF16)
        three = (rest - two.astype(F32)).astype(BF16)
        terms = jnp.where(lane < HEADS, one.astype(F32), jnp.where(lane < 2 * HEADS, two.astype(F32), three.astype(F32)))
        msg[n, :, WIDE:] = terms.astype(BF16)

    def m_copy(n, j):
        to = (c + j) % CTX
        src = msg.at[n, pl.ds(pl.multiple_of(to * PIECE, PIECE), PIECE)]
        return remote(src, rcv.at[j - 1, n], m_send.at[j - 1, n], m_recv.at[j - 1, n], s, to)

    def f_copy(n):
        dst = out_hbm.at[:, pl.ds(pl.multiple_of(group * WIDE, WIDE), WIDE)]
        return (
            remote(fin.at[n], dst, f_send.at[n], f_recv, f_seq(n), c),
            pltpu.make_async_copy(fin.at[n], dst, f_recv),
        )

    def join(n):
        for j in range(1, CTX):
            landed(rcv.at[j - 1, n], m_recv.at[j - 1, n])
        parts = [msg.at[n, rows_c]] + [rcv.at[j, n] for j in range(CTX - 1)]
        logs = []
        for part in parts:
            terms = part[:, WIDE:].astype(F32)
            logs.append(terms + pltpu.roll(terms, D - HEADS, 1) + pltpu.roll(terms, D - 2 * HEADS, 1))
        top = jnp.maximum(jnp.maximum(logs[0], logs[1]), jnp.maximum(logs[2], logs[3]))
        weights = [jnp.exp2(log - top) for log in logs]
        inverse = 1.0 / (weights[0] + weights[1] + weights[2] + weights[3])
        weights = [w * inverse for w in weights]
        for h in range(HEADS):
            cols = slice(h * D, (h + 1) * D)
            o = sum(part[:, cols].astype(F32) * w[:, h:h + 1] for part, w in zip(parts, weights))
            fin[n, :, cols] = o.astype(BF16)
        start_either(*f_copy(n), f_seq(n) == s)

    def send_parts(n):
        pack(n)
        for j in (2, 1, 3):
            m_copy(n, j).start()

    def kept_near(k, _):
        n = 2 * c + k

        @pl.when((n + NB - group) % NB < NEAR_AT)
        def _():
            acc[...] = kept[k]
            lse[...] = kept_lse[k]
            near(n)
            merge_near()
            send_parts(n)

        return 0

    def join_at(i, _):
        join(order(i))
        return 0

    def step(u, _):
        @pl.when(u == NEAR_AT)
        def _():
            pl.when(near_b > 0)(lambda: landed(kvn, kv_recv))
            pl.when(near_b == 0)(lambda: landed(kvn.at[pl.ds(KROWS, KROWS)], kv_recv))
            lax.fori_loop(0, 2, kept_near, 0)

        pl.when(u < NB - AHEAD)(lambda: forward(order(u + AHEAD)))

        @pl.when(u < NB)
        def _():
            n = order(u)
            for j in range(1, CTX):
                rows = pl.ds(pl.multiple_of(((c + CTX - j) % CTX) * PIECE, PIECE), PIECE)
                landed(q_buf.at[n, rows], y_recv.at[j - 1, n])
            is_near = n // 2 == c
            later = is_near & (u < NEAR_AT)
            attend(n)

            @pl.when(later)
            def _():
                kept[n % 2] = acc[...]
                kept_lse[n % 2] = lse[...]

            @pl.when(is_near & jnp.logical_not(later))
            def _():
                near(n)
                merge_near()

            pl.when(jnp.logical_not(later))(lambda: send_parts(n))

        first = u - LAG + jnp.where(u >= NB, 1, 0)

        @pl.when(u >= LAG)
        def _():
            lax.fori_loop(first, first + jnp.where(u == NB - 1, 2, 1), join_at, 0)

        return 0

    lax.fori_loop(0, NB + LAG - 1, step, 0)

    for j in range(1, HEADS):
        t_copy(j).wait_send()
    for g in range(8):
        there, _, own = q_copy(g)
        pl.when(jnp.logical_not(own))(there.wait_send)
        for role in range(2):
            there, _, _, other = kv_copy(role, g)
            pl.when(other)(there.wait_send)

    def drain(n, _):
        for j in range(1, CTX):
            y_copy(n, j).wait_send()
            m_copy(n, j).wait_send()
        pl.when(f_seq(n) != s)(f_copy(n)[0].wait_send)
        return 0

    lax.fori_loop(0, NB, drain, 0)
    landed(out_hbm, f_recv)


def body(queries, new_token_keys, new_token_values, cache_keys, cache_values, block_ids, block_counts):
    ids = block_ids[0].transpose(2, 1, 0)
    used = block_counts.transpose(0, 2, 1)
    blocks = cache_keys.shape[1] // KROWS
    hbm = pl.BlockSpec(memory_space=pltpu.MemorySpace.HBM)
    dma = pltpu.SemaphoreType.DMA
    return pl.pallas_call(
        kernel,
        out_shape=jax.ShapeDtypeStruct(queries.shape, BF16),
        in_specs=[hbm] * 7,
        out_specs=pl.BlockSpec(memory_space=pl.ANY),
        scratch_shapes=[
            pltpu.VMEM((NB, ROWS, WIDE), BF16),
            pltpu.VMEM((blocks, KROWS, D), BF16),
            pltpu.VMEM((blocks, KROWS, D), BF16),
            pltpu.VMEM((PIECE, WIDE), BF16),
            pltpu.VMEM((PIECE, WIDE), BF16),
            pltpu.VMEM((8, PIECE, 2 * D), BF16),
            pltpu.VMEM((2 * KROWS, 2 * D), BF16),
            pltpu.VMEM(ids.shape, jnp.int32),
            pltpu.VMEM(used.shape, jnp.int32),
            pltpu.VMEM((8, D), jnp.int32),
            pltpu.VMEM((HEADS, 8, D), jnp.int32),
            pltpu.SMEM((HEADS, 8, D), jnp.int32),
            pltpu.VMEM((HEADS, ROWS, KQ * KROWS), F32),
            pltpu.VMEM((ROWS, WIDE), F32),
            pltpu.VMEM((ROWS, D), F32),
            pltpu.VMEM((2, ROWS, WIDE), F32),
            pltpu.VMEM((2, ROWS, D), F32),
            pltpu.VMEM((ROWS, WIDE), F32),
            pltpu.VMEM((ROWS, D), F32),
            pltpu.VMEM((NB, ROWS, MSG), BF16),
            pltpu.VMEM((CTX - 1, NB, PIECE, MSG), BF16),
            pltpu.VMEM((NB, PIECE, WIDE), BF16),
            dma((6,)), dma((8,)), dma((NB,)), dma((CTX - 1, NB)), dma((CTX - 1, NB)), dma((16,)), dma, dma((HEADS,)), dma,
            dma((CTX - 1, NB)), dma((CTX - 1, NB)), dma((NB,)), dma, dma,
        ],
        compiler_params=pltpu.CompilerParams(
            collective_id=0, has_side_effects=True
        ),
        name="attend_all",
    )(
        queries, new_token_keys, new_token_values,
        cache_keys.reshape(blocks, KROWS, D), cache_values.reshape(blocks, KROWS, D), ids, used,
    )


def solution(mesh):
    return jax.shard_map(
        body,
        mesh=mesh,
        in_specs=(
            P(("seq", "ctx"), None),
            P(("seq", "ctx"), None),
            P(("seq", "ctx"), None),
            P("seq", "ctx", None),
            P("seq", "ctx", None),
            P("seq", None, "ctx", None),
            P("seq", None, "ctx"),
        ),
        out_specs=P(("seq", "ctx"), None),
        check_vma=False,
    )
```
